32 devices in a mesh: rep: 16 (over z, x, core), fsdp: 2 (over y).
Axes of the slice: x: 2, y: 2, z: 4, core: 2. Of those that a mesh axis runs over, the one named last changes fastest.
Arguments:
- gradients: bfloat16 [16, 4, 64, 4096], P('rep', None, 'fsdp'), may hold values from -8000 to 8000
- local_params: float32 [16, 4, 64, 4096], P('rep', None, 'fsdp'), may hold values from -6 to 6
- first_moment: float32 [16, 4, 64, 4096], P('rep', None, 'fsdp'), may hold values from -6 to 6
- second_moment: float32 [16, 4, 64, 4096], P('rep', None, 'fsdp'), may hold values from 0.05 to 2
- global_params: float32 [4, 64, 4096], P(None, 'fsdp'), may hold values from -6 to 6
- outer_momentum: float32 [4, 64, 4096], P(None, 'fsdp'), may hold values from -6 to 6
Outputs:
- new_global: float32 [4, 64, 4096], P(None, 'fsdp')
- new_momentum: float32 [4, 64, 4096], P(None, 'fsdp')
- new_first: float32 [16, 4, 64, 4096], P('rep', None, 'fsdp')
- new_second: float32 [16, 4, 64, 4096], P('rep', None, 'fsdp')
The draws below stay inside these ranges and needn't reach their ends.
All inputs are finite; a program needn't handle non-finite values.
Results may differ from the reference program's by a relative error of at most 0.0003.
Values sent between devices are 32-bit elements; how exact they have to be, the bound alone decides.
A program may use at most 128 MiB of HBM per device.

```python
import math
import jax
import jax.numpy as jnp
from jax import lax

D = 4096
MATRICES = 4
STEP = 20
ROWS = 64
REPLICAS = 16


def draw_gradients(key, part):
    keys = jax.random.split(key, 5)
    shape = (REPLICAS, MATRICES, ROWS, D)
    base = jnp.clip(jax.random.normal(keys[0], shape, jnp.float32), -6.0, 6.0)
    power = 1.0
    row_scale = jnp.exp(jax.random.uniform(keys[1], (REPLICAS, MATRICES, ROWS, 1), jnp.float32) * math.log(10.0))
    col_scale = jnp.exp(jax.random.uniform(keys[2], (REPLICAS, MATRICES, 1, D), jnp.float32) * math.log(10.0))
    ramp = 1.0 + 2.0 * jnp.arange(ROWS, dtype=jnp.float32) / max(ROWS - 1, 1)
    ramp = (ramp ** power).reshape(1, 1, ROWS, 1)
    values = base * row_scale * col_scale * ramp
    order = jax.random.permutation(keys[4], REPLICAS)
    quiet = (order < REPLICAS // 4).astype(jnp.float32).reshape(REPLICAS, 1, 1, 1)
    values = values * (1.0 - 0.999 * quiet)
    return jnp.clip(values, -8000.0, 8000.0).astype(jnp.bfloat16)


def block_levels(rng, shape, shards, low, largest):
    def one(axis_at, shards_of):
        steps = jax.random.uniform(jax.random.fold_in(jax.random.fold_in(rng, 6), axis_at), (shards_of,), jnp.float32, low / len(shards), largest / len(shards))
        return jnp.repeat(jnp.exp(steps), shape[axis_at] // shards_of).reshape((-1,) + (1,) * (len(shape) - axis_at - 1))

    level = one(*shards[0])
    for cut in shards[1:]:
        level = level * one(*cut)
    return level


def bell_draw(stream_key, dims, deviation, bound, cuts=(), kind=jnp.bfloat16):
    entries = jax.random.normal(stream_key, dims, jnp.float32) * deviation
    if len(cuts) > 0:
        entries = block_levels(stream_key, dims, cuts, -0.22, 0.18) * entries
    return jnp.clip(entries, min=-bound, max=bound).astype(kind)


def setup_inputs(seed: int = 0) -> dict:
    key_list = jax.random.split(jax.random.key(seed), 7)
    gradients = draw_gradients(jax.random.fold_in(key_list[6], 71), 0)
    local_params = bell_draw(key_list[1], (REPLICAS, MATRICES, ROWS, D), 1.0, 6.0, ((0, 16), (2, 2)), jnp.float32)
    first_moment = bell_draw(key_list[2], (REPLICAS, MATRICES, ROWS, D), 0.5, 6.0, ((0, 16), (2, 2)), jnp.float32)
    second_moment = jnp.clip(jnp.exp(math.log(2.0) - 3.6888794 * jax.random.uniform(key_list[3], (REPLICAS, MATRICES, ROWS, D), jnp.float32) ** block_levels(key_list[3], (REPLICAS, MATRICES, ROWS, D), ((0, 16), (2, 2)), -0.2, 0.2)), 0.05, 2.0)
    global_params = bell_draw(key_list[4], (MATRICES, ROWS, D), 1.0, 6.0, ((1, 2),), jnp.float32)
    outer_momentum = bell_draw(key_list[5], (MATRICES, ROWS, D), 0.5, 6.0, ((1, 2),), jnp.float32)
    return dict(gradients=gradients, local_params=local_params, first_moment=first_moment, second_moment=second_moment, global_params=global_params, outer_momentum=outer_momentum)


def reference(gradients, local_params, first_moment, second_moment, global_params, outer_momentum):
    first_fix = 1.0 - 0.9 ** STEP
    second_fix = 1.0 - 0.95 ** STEP

    def one_replica(carry, items):
        gradient, local_now, moment_one, moment_two = items
        gradient = gradient.astype(jnp.float32)
        squares = jnp.sum(gradient * gradient)
        rms_value = jnp.sqrt(squares / (MATRICES * ROWS * D))
        factor = jnp.minimum(1.0, 0.5 / rms_value)
        clipped = gradient * factor
        first_new = 0.9 * moment_one + 0.1 * clipped
        second_new = 0.95 * moment_two + 0.05 * clipped * clipped
        update = first_new / first_fix / (jnp.sqrt(second_new / second_fix) + 1e-08)
        stepped = local_now - 0.1 * (update + 0.1 * local_now)
        carry = carry + (global_params - stepped)
        return (carry, (first_new, second_new))
    start = jnp.zeros(global_params.shape, jnp.float32)
    total, (first_all, second_all) = lax.scan(one_replica, start, (gradients, local_params, first_moment, second_moment))
    pseudo = total / REPLICAS
    momentum_next = 0.9 * outer_momentum + pseudo
    global_next = global_params - 0.7 * (pseudo + 0.9 * momentum_next)
    return (global_next, momentum_next, first_all, second_all)
```

```python
import functools

import jax
import jax.numpy as jnp
from jax import lax
from jax.experimental import pallas as pl
from jax.experimental.pallas import tpu as pltpu
from jax.sharding import PartitionSpec as P

STEP = 20
FIRST_FIX = 1.0 - 0.9**STEP
SECOND_FIX = 1.0 - 0.95**STEP
CHUNKS = 4
MESH = pl.DeviceIdType.MESH


def kernel(shape, g_hbm, p_hbm, f_hbm, s_hbm, mean_hbm, factor_ref,
           g, p, f, s, delta, recv_c, part_x, recv_x, part_z, recv_z, res, squares,
           load_sem, sq_send, sq_recv, c_send, c_recv, x_send, x_recv, z_send, z_recv,
           gz_send, gz_recv, gx_send, gx_recv, gc_send, gc_recv, out_sem):
    reps, peers, depth = shape
    rows, width = delta.shape[3], delta.shape[4]
    chunks = delta.shape[0]
    me = lax.axis_index("rep")
    fs = lax.axis_index("fsdp")
    core = lax.rem(me, 2)
    x = lax.rem(me // 2, 2)
    z = me // 4
    mine = 2 * core + x
    other_core = {"rep": me + 1 - 2 * core}
    other_x = {"rep": me + 2 - 4 * x}

    def along_z(d):
        return {"rep": lax.rem(z + d, depth) * 4 + mine_id}

    mine_id = lax.rem(me, 4)

    loads = [pltpu.make_async_copy(src, dst, load_sem.at[i])
             for i, (src, dst) in enumerate(((g_hbm, g), (f_hbm, f), (s_hbm, s), (p_hbm, p)))]
    for load in loads:
        load.start()

    barrier = pltpu.get_barrier_semaphore()
    pl.semaphore_signal(barrier, inc=1, device_id=other_core, device_id_type=MESH)
    pl.semaphore_signal(barrier, inc=1, device_id=other_x, device_id_type=MESH)
    for d in range(1, depth):
        pl.semaphore_signal(barrier, inc=1, device_id=along_z(d), device_id_type=MESH)
    for d in range(1, peers):
        pl.semaphore_signal(barrier, inc=1, device_id={"fsdp": lax.rem(fs + d, peers)}, device_id_type=MESH)

    loads[0].wait()
    step = 512
    per = g.shape[2] // step

    def square(i, acc):
        part = g[i // per, :, pl.ds(pl.multiple_of(lax.rem(i, per) * step, step), step)].astype(jnp.float32)
        return acc + part * part

    acc = lax.fori_loop(0, g.shape[0] * per, square, jnp.zeros((rows, step), jnp.float32))
    acc = sum(acc[:, i * 128:(i + 1) * 128] for i in range(step // 128))
    squares[0] = sum(acc[i * 8:(i + 1) * 8] for i in range(rows // 8))

    pl.semaphore_wait(barrier, 2 + depth - 1 + peers - 1)
    sq = []
    for d in range(1, peers):
        copy = pltpu.make_async_remote_copy(
            squares.at[0], squares.at[d], sq_send.at[d], sq_recv.at[d],
            device_id={"fsdp": lax.rem(fs + d, peers)}, device_id_type=MESH)
        copy.start()
        sq.append(copy)
    for copy in sq:
        copy.wait()
    total = squares[0]
    for d in range(1, peers):
        total = total + squares[d]
    mean_sq = jnp.sum(total, keepdims=True) / (g.shape[0] * rows * g.shape[2] * peers)
    factor = jnp.where(mean_sq > 0.25, 0.5 / jnp.sqrt(mean_sq), 1.0)
    factor_ref[...] = jnp.broadcast_to(factor, factor_ref.shape)
    for load in loads[1:]:
        load.wait()

    def columns(k, zz):
        return pl.ds(pl.multiple_of((k * depth + zz) * width, width), width)

    def half(k, which):
        def piece(i, _):
            m = 2 * which + i // depth
            zz = lax.rem(i, depth)
            at = columns(k, zz)
            clipped = g[m, :, at].astype(jnp.float32) * factor
            first = 0.9 * f[m, :, at] + 0.1 * clipped
            second = 0.95 * s[m, :, at] + 0.05 * clipped * clipped
            update = (first * (0.1 / FIRST_FIX)) / (jnp.sqrt(second * (1.0 / SECOND_FIX)) + 1e-8)
            delta[k, m, zz] = 0.99 * p[m, :, at] - update
            return 0
        lax.fori_loop(0, 2 * depth, piece, 0)

    def remote(src, dst, send, recv, where):
        return pltpu.make_async_remote_copy(src, dst, send, recv, device_id=where, device_id_type=MESH)

    def c_copy(k):
        return remote(delta.at[k, pl.ds(2 * (1 - core), 2)], recv_c.at[k], c_send.at[k], c_recv.at[k], other_core)

    def x_copy(k):
        return remote(part_x.at[k], recv_x.at[k], x_send.at[k], x_recv.at[k], other_x)

    def z_copy(k, d):
        return remote(part_z.at[k, lax.rem(z + d, depth)], recv_z.at[k, d], z_send.at[k, d], z_recv.at[k, d], along_z(d))

    def gz_copy(k, d):
        return remote(res.at[k, mine, z], res.at[k, mine, z], gz_send.at[k, d], gz_recv.at[k, d], along_z(d))

    def gx_copy(k):
        return remote(res.at[k, mine], res.at[k, mine], gx_send.at[k], gx_recv.at[k], other_x)

    def gc_copy(k):
        own = res.at[k, pl.ds(2 * core, 2)]
        return remote(own, own, gc_send.at[k], gc_recv.at[k], other_core)

    def out_copy(k, m, zz):
        return pltpu.make_async_copy(res.at[k, m, zz], mean_hbm.at[m, :, columns(k, zz)], out_sem.at[k, m, zz])

    def compute(k):
        half(k, 1 - core)
        c_copy(k).start()
        half(k, core)

    def reduce_core(k):
        c_copy(k).wait_recv()

        def piece(i, _):
            part_x[k, i] = delta[k, 2 * core + 1 - x, i] + recv_c[k, 1 - x, i]
            return 0
        lax.fori_loop(0, depth, piece, 0)
        x_copy(k).start()

    def reduce_x(k):
        x_copy(k).wait_recv()

        def piece(i, _):
            part_z[k, i] = delta[k, mine, i] + recv_c[k, x, i] + recv_x[k, i]
            return 0
        lax.fori_loop(0, depth, piece, 0)
        for d in range(1, depth):
            z_copy(k, d).start()

    def reduce_z(k):
        for d in range(1, depth):
            z_copy(k, d).wait_recv()
        total = part_z[k, z]
        for d in range(1, depth):
            total = total + recv_z[k, d]
        res[k, mine, z] = total * (1.0 / reps)
        for d in range(1, depth):
            gz_copy(k, d).start()

    def gather_z(k):
        for d in range(1, depth):
            gz_copy(k, d).wait_recv()
        gx_copy(k).start()

    def gather_x(k):
        gx_copy(k).wait_recv()
        gc_copy(k).start()

    def gather_core(k):
        gc_copy(k).wait_recv()
        for m in range(4):
            for zz in range(depth):
                out_copy(k, m, zz).start()

    for k in range(chunks):
        compute(k)
        if k:
            reduce_core(k - 1)
    reduce_core(chunks - 1)
    stages = (reduce_x, reduce_z, gather_z, gather_x, gather_core)
    for t in range(chunks + len(stages) - 1):
        for i, stage in enumerate(stages):
            if 0 <= t - i < chunks:
                stage(t - i)
    for k in range(chunks):
        c_copy(k).wait_send()
        x_copy(k).wait_send()
        gx_copy(k).wait_send()
        gc_copy(k).wait_send()
        for d in range(1, depth):
            z_copy(k, d).wait_send()
            gz_copy(k, d).wait_send()
        for m in range(4):
            for zz in range(depth):
                out_copy(k, m, zz).wait()


def on_device(gradients, local_params, first_moment, second_moment, global_params, outer_momentum):
    reps, peers = lax.axis_size("rep"), lax.axis_size("fsdp")
    depth = reps // 4
    matrices, rows, d = global_params.shape
    width = d // (CHUNKS * depth)
    f32 = jnp.float32
    piece = (rows, width)
    dma = pltpu.SemaphoreType.DMA
    block = (matrices, rows, d)
    any_spec = pl.BlockSpec(memory_space=pl.ANY)
    mean, factor = pl.pallas_call(
        functools.partial(kernel, (reps, peers, depth)),
        out_shape=(jax.ShapeDtypeStruct(block, f32), jax.ShapeDtypeStruct((8, 128), f32)),
        in_specs=[any_spec] * 4,
        out_specs=(any_spec, pl.BlockSpec(memory_space=pltpu.VMEM)),
        scratch_shapes=[
            pltpu.VMEM(block, gradients.dtype), pltpu.VMEM(block, f32), pltpu.VMEM(block, f32), pltpu.VMEM(block, f32),
            pltpu.VMEM((CHUNKS, 4, depth) + piece, f32),
            pltpu.VMEM((CHUNKS, 2, depth) + piece, f32),
            pltpu.VMEM((CHUNKS, depth) + piece, f32),
            pltpu.VMEM((CHUNKS, depth) + piece, f32),
            pltpu.VMEM((CHUNKS, depth) + piece, f32),
            pltpu.VMEM((CHUNKS, depth) + piece, f32),
            pltpu.VMEM((CHUNKS, 4, depth) + piece, f32),
            pltpu.VMEM((peers, 8, 128), f32),
            dma((4,)), dma((peers,)), dma((peers,)),
            dma((CHUNKS,)), dma((CHUNKS,)), dma((CHUNKS,)), dma((CHUNKS,)),
            dma((CHUNKS, depth)), dma((CHUNKS, depth)), dma((CHUNKS, depth)), dma((CHUNKS, depth)),
            dma((CHUNKS,)), dma((CHUNKS,)), dma((CHUNKS,)), dma((CHUNKS,)),
            dma((CHUNKS, 4, depth)),
        ],
        compiler_params=pltpu.CompilerParams(
            collective_id=0, has_side_effects=True, vmem_limit_bytes=40 * 1024 * 1024),
    )(gradients.reshape(block), local_params.reshape(block), first_moment.reshape(block), second_moment.reshape(block))
    clipped = gradients.astype(f32) * factor[0, 0]
    first_new = 0.9 * first_moment + 0.1 * clipped
    second_new = 0.95 * second_moment + 0.05 * clipped * clipped
    pseudo = global_params - mean
    momentum_next = 0.9 * outer_momentum + pseudo
    global_next = global_params - 0.7 * (pseudo + 0.9 * momentum_next)
    return (global_next, momentum_next, first_new, second_new)


def solution(mesh):
    placed = (
        P("rep", None, "fsdp", None),
        P("rep", None, "fsdp", None),
        P("rep", None, "fsdp", None),
        P("rep", None, "fsdp", None),
        P(None, "fsdp", None),
        P(None, "fsdp", None),
    )
    return jax.shard_map(
        on_device,
        mesh=mesh,
        in_specs=placed,
        out_specs=(
            P(None, "fsdp", None),
            P(None, "fsdp", None),
            P("rep", None, "fsdp", None),
            P("rep", None, "fsdp", None),
        ),
        check_vma=False,
    )
```

```python
import functools

import jax
import jax.numpy as jnp
from jax import lax
from jax.experimental import pallas as pl
from jax.experimental.pallas import tpu as pltpu
from jax.sharding import PartitionSpec as P

STEP = 20
FIRST_FIX = 1.0 - 0.9**STEP
SECOND_FIX = 1.0 - 0.95**STEP
CHUNKS = 4
MESH = pl.DeviceIdType.MESH


def kernel(shape, g_hbm, p_hbm, f_hbm, s_hbm, w_hbm, v_hbm, new_w, new_v, new_f, new_s,
           g, p, f, s, w, v, delta, recv_c, part_x, recv_x, part_z, recv_z, res, squares,
           load_sem, sq_send, sq_recv, c_send, c_recv, x_send, x_recv, z_send, z_recv,
           gz_send, gz_recv, gx_send, gx_recv, gc_send, gc_recv, out_sem):
    reps, peers, depth = shape
    rows, width = delta.shape[3], delta.shape[4]
    chunks = delta.shape[0]
    me = lax.axis_index("rep")
    fs = lax.axis_index("fsdp")
    core = lax.rem(me, 2)
    x = lax.rem(me // 2, 2)
    z = me // 4
    mine = 2 * core + x
    other_core = {"rep": me + 1 - 2 * core}
    other_x = {"rep": me + 2 - 4 * x}

    def along_z(d):
        return {"rep": lax.rem(z + d, depth) * 4 + mine_id}

    mine_id = lax.rem(me, 4)

    loads = [pltpu.make_async_copy(src, dst, load_sem.at[i])
             for i, (src, dst) in enumerate(((g_hbm, g), (f_hbm, f), (s_hbm, s), (p_hbm, p), (w_hbm, w), (v_hbm, v)))]
    for load in loads:
        load.start()

    barrier = pltpu.get_barrier_semaphore()
    pl.semaphore_signal(barrier, inc=1, device_id=other_core, device_id_type=MESH)
    pl.semaphore_signal(barrier, inc=1, device_id=other_x, device_id_type=MESH)
    for d in range(1, depth):
        pl.semaphore_signal(barrier, inc=1, device_id=along_z(d), device_id_type=MESH)
    for d in range(1, peers):
        pl.semaphore_signal(barrier, inc=1, device_id={"fsdp": lax.rem(fs + d, peers)}, device_id_type=MESH)

    loads[0].wait()
    step = 512
    per = g.shape[2] // step

    def square(i, acc):
        part = g[i // per, :, pl.ds(pl.multiple_of(lax.rem(i, per) * step, step), step)].astype(jnp.float32)
        return acc + part * part

    acc = lax.fori_loop(0, g.shape[0] * per, square, jnp.zeros((rows, step), jnp.float32))
    acc = sum(acc[:, i * 128:(i + 1) * 128] for i in range(step // 128))
    squares[0] = sum(acc[i * 8:(i + 1) * 8] for i in range(rows // 8))

    pl.semaphore_wait(barrier, 2 + depth - 1 + peers - 1)
    sq = []
    for d in range(1, peers):
        copy = pltpu.make_async_remote_copy(
            squares.at[0], squares.at[d], sq_send.at[d], sq_recv.at[d],
            device_id={"fsdp": lax.rem(fs + d, peers)}, device_id_type=MESH)
        copy.start()
        sq.append(copy)
    for copy in sq:
        copy.wait()
    total = squares[0]
    for d in range(1, peers):
        total = total + squares[d]
    mean_sq = jnp.sum(total, keepdims=True) / (g.shape[0] * rows * g.shape[2] * peers)
    factor = jnp.where(mean_sq > 0.25, 0.5 / jnp.sqrt(mean_sq), 1.0)
    for load in loads[1:4]:
        load.wait()

    def columns(k, zz):
        return pl.ds(pl.multiple_of((k * depth + zz) * width, width), width)

    def half(k, which):
        def piece(i, _):
            m = 2 * which + i // depth
            zz = lax.rem(i, depth)
            at = columns(k, zz)
            clipped = g[m, :, at].astype(jnp.float32) * factor
            first = 0.9 * f[m, :, at] + 0.1 * clipped
            second = 0.95 * s[m, :, at] + 0.05 * clipped * clipped
            f[m, :, at] = first
            s[m, :, at] = second
            update = (first * (0.1 / FIRST_FIX)) / (jnp.sqrt(second * (1.0 / SECOND_FIX)) + 1e-8)
            delta[k, m, zz] = 0.99 * p[m, :, at] - update
            return 0
        lax.fori_loop(0, 2 * depth, piece, 0)

    def remote(src, dst, send, recv, where):
        return pltpu.make_async_remote_copy(src, dst, send, recv, device_id=where, device_id_type=MESH)

    def c_copy(k):
        return remote(delta.at[k, pl.ds(2 * (1 - core), 2)], recv_c.at[k], c_send.at[k], c_recv.at[k], other_core)

    def x_copy(k):
        return remote(part_x.at[k], recv_x.at[k], x_send.at[k], x_recv.at[k], other_x)

    def z_copy(k, d):
        return remote(part_z.at[k, lax.rem(z + d, depth)], recv_z.at[k, d], z_send.at[k, d], z_recv.at[k, d], along_z(d))

    def gz_copy(k, d):
        return remote(res.at[k, mine, z], res.at[k, mine, z], gz_send.at[k, d], gz_recv.at[k, d], along_z(d))

    def gx_copy(k):
        return remote(res.at[k, mine], res.at[k, mine], gx_send.at[k], gx_recv.at[k], other_x)

    def gc_copy(k):
        own = res.at[k, pl.ds(2 * core, 2)]
        return remote(own, own, gc_send.at[k], gc_recv.at[k], other_core)

    def out_copies(k):
        at = pl.ds(k * depth * width, depth * width)
        return [pltpu.make_async_copy(src.at[:, :, at], dst.at[:, :, at], out_sem.at[i, k])
                for i, (src, dst) in enumerate(((w, new_w), (v, new_v)))]

    moments = [pltpu.make_async_copy(src, dst, load_sem.at[i])
               for i, (src, dst) in enumerate(((f, new_f), (s, new_s)))]

    def compute(k):
        half(k, 1 - core)
        c_copy(k).start()
        half(k, core)

    def reduce_core(k):
        c_copy(k).wait_recv()

        def piece(i, _):
            part_x[k, i] = delta[k, 2 * core + 1 - x, i] + recv_c[k, 1 - x, i]
            return 0
        lax.fori_loop(0, depth, piece, 0)
        x_copy(k).start()

    def reduce_x(k):
        x_copy(k).wait_recv()

        def piece(i, _):
            part_z[k, i] = delta[k, mine, i] + recv_c[k, x, i] + recv_x[k, i]
            return 0
        lax.fori_loop(0, depth, piece, 0)
        for d in range(1, depth):
            z_copy(k, d).start()

    def reduce_z(k):
        for d in range(1, depth):
            z_copy(k, d).wait_recv()
        total = part_z[k, z]
        for d in range(1, depth):
            total = total + recv_z[k, d]
        res[k, mine, z] = total * (1.0 / reps)
        for d in range(1, depth):
            gz_copy(k, d).start()

    def gather_z(k):
        for d in range(1, depth):
            gz_copy(k, d).wait_recv()
        gx_copy(k).start()

    def gather_x(k):
        gx_copy(k).wait_recv()
        gc_copy(k).start()

    def gather_core(k):
        gc_copy(k).wait_recv()

        def piece(i, _):
            m = i // depth
            zz = lax.rem(i, depth)
            at = columns(k, zz)
            now = w[m, :, at]
            pseudo = now - res[k, m, zz]
            momentum = 0.9 * v[m, :, at] + pseudo
            v[m, :, at] = momentum
            w[m, :, at] = now - 0.7 * (pseudo + 0.9 * momentum)
            return 0
        lax.fori_loop(0, 4 * depth, piece, 0)
        for copy in out_copies(k):
            copy.start()

    for k in range(chunks):
        compute(k)
        if k:
            reduce_core(k - 1)
    reduce_core(chunks - 1)
    for copy in moments:
        copy.start()
    for load in loads[4:]:
        load.wait()
    stages = (reduce_x, reduce_z, gather_z, gather_x, gather_core)
    for t in range(chunks + len(stages) - 1):
        for i, stage in enumerate(stages):
            if 0 <= t - i < chunks:
                stage(t - i)
    for k in range(chunks):
        c_copy(k).wait_send()
        x_copy(k).wait_send()
        gx_copy(k).wait_send()
        gc_copy(k).wait_send()
        for d in range(1, depth):
            z_copy(k, d).wait_send()
            gz_copy(k, d).wait_send()
        for copy in out_copies(k):
            copy.wait()
    for copy in moments:
        copy.wait()


def on_device(gradients, local_params, first_moment, second_moment, global_params, outer_momentum):
    reps, peers = lax.axis_size("rep"), lax.axis_size("fsdp")
    depth = reps // 4
    matrices, rows, d = global_params.shape
    width = d // (CHUNKS * depth)
    f32 = jnp.float32
    piece = (rows, width)
    dma = pltpu.SemaphoreType.DMA
    block = (matrices, rows, d)
    outs = pl.pallas_call(
        functools.partial(kernel, (reps, peers, depth)),
        out_shape=(jax.ShapeDtypeStruct(block, f32),) * 4,
        in_specs=[pl.BlockSpec(memory_space=pltpu.HBM)] * 6,
        out_specs=(pl.BlockSpec(memory_space=pl.ANY),) * 4,
        scratch_shapes=[
            pltpu.VMEM(block, gradients.dtype), *[pltpu.VMEM(block, f32)] * 5,
            pltpu.VMEM((CHUNKS, 4, depth) + piece, f32),
            pltpu.VMEM((CHUNKS, 2, depth) + piece, f32),
            pltpu.VMEM((CHUNKS, depth) + piece, f32),
            pltpu.VMEM((CHUNKS, depth) + piece, f32),
            pltpu.VMEM((CHUNKS, depth) + piece, f32),
            pltpu.VMEM((CHUNKS, depth) + piece, f32),
            pltpu.VMEM((CHUNKS, 4, depth) + piece, f32),
            pltpu.VMEM((peers, 8, 128), f32),
            dma((6,)), dma((peers,)), dma((peers,)),
            dma((CHUNKS,)), dma((CHUNKS,)), dma((CHUNKS,)), dma((CHUNKS,)),
            dma((CHUNKS, depth)), dma((CHUNKS, depth)), dma((CHUNKS, depth)), dma((CHUNKS, depth)),
            dma((CHUNKS,)), dma((CHUNKS,)), dma((CHUNKS,)), dma((CHUNKS,)),
            dma((2, CHUNKS)),
        ],
        compiler_params=pltpu.CompilerParams(
            collective_id=0, has_side_effects=True, vmem_limit_bytes=28 * 1024 * 1024),
    )(*[pltpu.with_memory_space_constraint(a.reshape(block), pltpu.HBM)
        for a in (gradients, local_params, first_moment, second_moment, global_params, outer_momentum)])
    return (outs[0], outs[1], outs[2][None], outs[3][None])


def solution(mesh):
    placed = (
        P("rep", None, "fsdp", None),
        P("rep", None, "fsdp", None),
        P("rep", None, "fsdp", None),
        P("rep", None, "fsdp", None),
        P(None, "fsdp", None),
        P(None, "fsdp", None),
    )
    return jax.shard_map(
        on_device,
        mesh=mesh,
        in_specs=placed,
        out_specs=(
            P(None, "fsdp", None),
            P(None, "fsdp", None),
            P("rep", None, "fsdp", None),
            P("rep", None, "fsdp", None),
        ),
        check_vma=False,
    )
```
